256 devices in a mesh: dp: 8 (over z), seq: 32 (over x, y, core).
Axes of the slice: x: 4, y: 4, z: 8, core: 2. Of those that a mesh axis runs over, the one named last changes fastest.
Arguments:
- tokens: bfloat16 [128, 4, 2560], P('dp'), may hold values from -6 to 6
- attn_gain: float32 [2560], replicated, may hold values from 0.1 to 1.9
- qkv_weight: bfloat16 [3072, 2560], P(('seq', 'dp'))
- out_weight: bfloat16 [2560, 2560], P(('seq', 'dp')), may hold values from -0.125 to 0.125
- mlp_gain: float32 [2560], replicated, may hold values from 0.1 to 1.9
- gate_up: bfloat16 [2, 7680, 2560], P(None, 'seq'), may hold values from -0.125 to 0.125
- down_weight: bfloat16 [7680, 2560], P('seq'), may hold values from -0.0625 to 0.0625
- kv_pool: bfloat16 [4096, 128, 512], P(('dp', 'seq')), may hold values from -6 to 6
- cache_len: int32 [128], P('dp'), may hold values from 1 to 16384, as said below
- page_table: int32 [128, 16], P('dp'), may hold values from 0 to 511, as said below
Outputs:
- layer_out: bfloat16 [128, 4, 2560], P('dp')
- written_pool: bfloat16 [4096, 128, 512], P(('dp', 'seq'))
The draws below stay inside these ranges and needn't reach their ends.
Inputs may be any that keep to these rules, and one draw needn't show every extreme that they name: `cache_len`: some request of the whole batch has exactly 16384 cached tokens; lengths under 2048 occur. `page_table`: within the 16 requests of one dp index all entries differ. Slot s lies on seq index s // 16; in every dp index some seq index holds exactly 16 of its pages.
All inputs are finite; a program needn't handle non-finite values.
Results may differ from the reference program's by a relative error of at most 0.018.
Values may be sent and summed in bfloat16 or wider, within the bound.
A program may use at most 128 MiB of HBM per device.

```python
import jax
import jax.numpy as jnp
from jax import lax

D = 2560
H = 10
HD = 256
FF = 7680
WIN = 2048
PAGE = 128
NEW = 4
MAXLEN = 16384
R_DEV = 16
NP = 16
REQ = 128
P_DEV = 16
POOL = 4096
N_SEQ = 32


def draw_qkv_weight(key, part):
    first_key = jax.random.fold_in(key, 0)
    spread = D ** (-0.5)
    return (jax.random.normal(first_key, ((H + 2) * HD, D), jnp.float32) * spread).astype(jnp.bfloat16)


def draw_cache_len(key, part):
    pick_key, short_key, long_key, spot_key = jax.random.split(key, 4)
    short_len = jax.random.randint(short_key, (REQ,), 1, WIN + 1)
    long_len = jax.random.randint(long_key, (REQ,), WIN, MAXLEN + 1)
    lengths = jnp.where(jax.random.randint(pick_key, (REQ,), 0, 2) == 0, short_len, long_len)
    chosen = jax.random.randint(spot_key, (), 0, REQ)
    return jnp.where(jnp.arange(REQ) == chosen, MAXLEN, lengths).astype(jnp.int32)


def draw_page_table(key, part):
    group_slots = P_DEV * N_SEQ
    wanted = R_DEV * NP

    def one_group(group_key):
        bias_key, hot_key, noise_key, order_key = jax.random.split(group_key, 4)
        bias = jax.random.randint(bias_key, (N_SEQ,), 0, 4)
        hottest = jax.random.randint(hot_key, (), 0, N_SEQ)
        bias = jnp.where(jnp.arange(N_SEQ) == hottest, 8, bias)
        noise = jax.random.randint(noise_key, (group_slots,), 0, 1024)
        slot_ids = jnp.arange(group_slots, dtype=jnp.int32)
        owner_dev = slot_ids // P_DEV
        score = (bias[owner_dev] * 1024 + noise) * group_slots + slot_ids
        unused, picked = lax.top_k(score, wanted)
        shuffled = jax.random.permutation(order_key, picked)
        return shuffled.reshape(R_DEV, NP).astype(jnp.int32)
    group_keys = jax.random.split(key, REQ // R_DEV)
    return jax.vmap(one_group)(group_keys).reshape(REQ, NP).astype(jnp.int32)


def levels(own_key, dims, pieces, low, top_value):
    def one(position, blocks):
        heights = jax.random.uniform(jax.random.fold_in(jax.random.fold_in(own_key, 6), position), (blocks,), jnp.float32, low / len(pieces), top_value / len(pieces))
        return jnp.repeat(jnp.exp(heights), dims[position] // blocks).reshape((-1,) + (1,) * (len(dims) - position - 1))

    level = one(*pieces[0])
    for cut in pieces[1:]:
        level = level * one(*cut)
    return level


def scatter_about(own_key, shape, deviation, limit, pieces=(), kind=jnp.bfloat16):
    entries = jax.random.normal(own_key, shape, jnp.float32) * deviation
    if len(pieces) > 0:
        entries = levels(own_key, shape, pieces, -0.22, 0.18) * entries
    return jnp.clip(entries, min=-limit, max=limit).astype(kind)


def setup_inputs(seed: int = 0) -> dict:
    keys = jax.random.split(jax.random.key(seed), 11)
    return {
        "tokens": scatter_about(keys[0], (REQ, NEW, D), 1.0, 6.0, ((0, 8),)),
        "attn_gain": jnp.clip(1.0 + 0.18 * jax.random.normal(keys[1], (D,), jnp.float32), 0.1, 1.9),
        "qkv_weight": draw_qkv_weight(jax.random.fold_in(keys[10], 71), 0),
        "out_weight": scatter_about(keys[3], (D, H * HD), (H * HD) ** -0.5, 0.125, ((0, 256),)),
        "mlp_gain": jnp.clip(1.0 + 0.18 * jax.random.normal(keys[4], (D,), jnp.float32), 0.1, 1.9),
        "gate_up": scatter_about(keys[5], (2, FF, D), D ** -0.5, 0.125, ((1, 32),)),
        "down_weight": scatter_about(keys[6], (FF, D), FF ** -0.5, 0.0625, ((0, 32),)),
        "kv_pool": scatter_about(keys[7], (POOL, PAGE, 2 * HD), 1.0, 6.0, ((0, 256),)),
        "cache_len": draw_cache_len(jax.random.fold_in(keys[10], 71), 0),
        "page_table": draw_page_table(jax.random.fold_in(keys[10], 71), 0),
    }


def rms_norm(values, gains):
    floats = values.astype(jnp.float32)
    return floats * lax.rsqrt(lax.optimization_barrier(jnp.mean(floats * floats, axis=-1, keepdims=True)) + 1e-06) * gains

def rotate(values, positions):
    quarter = values.shape[-1] // 4
    freq_index = jnp.arange(quarter).astype(jnp.float32)
    inverse = 10000.0 ** (-freq_index / quarter)
    angles = positions[..., None] * inverse
    first = values[..., :quarter]
    second = values[..., quarter:2 * quarter]
    others = values[..., 2 * quarter:]
    cosine = jnp.cos(angles)
    sine = jnp.sin(angles)
    return jnp.concatenate([first * cosine - second * sine, second * cosine + first * sine, others], axis=-1)

def reference(tokens, attn_gain, qkv_weight, out_weight, mlp_gain, gate_up, down_weight, kv_pool, cache_len, page_table):
    group_slots = P_DEV * N_SEQ
    scale = HD ** (-0.5)
    normed = rms_norm(tokens, attn_gain).astype(jnp.bfloat16).reshape(REQ * NEW, D)
    projected = jnp.dot(normed, qkv_weight.T, preferred_element_type=jnp.float32).astype(jnp.bfloat16)
    projected = projected.reshape(REQ, NEW, (H + 2) * HD)
    positions_int = cache_len[:, None] + jnp.arange(NEW, dtype=jnp.int32)[None, :]
    positions = positions_int.astype(jnp.float32)
    queries = rotate(projected[:, :, :H * HD].astype(jnp.float32).reshape(REQ, NEW, H, HD), positions[:, :, None]).astype(jnp.bfloat16)
    keys_new = rotate(projected[:, :, H * HD:(H + 1) * HD].astype(jnp.float32), positions).astype(jnp.bfloat16)
    values_new = projected[:, :, (H + 1) * HD:]

    def attend(request):
        group = request // R_DEV
        rows_index = group * group_slots + page_table[request]
        cached = kv_pool[rows_index].reshape(WIN, 2 * HD)
        length = cache_len[request]
        cycle = jnp.arange(WIN, dtype=jnp.int32)
        key_pos = length - 1 - jnp.mod(length - 1 - cycle, WIN)
        query_pos = length + jnp.arange(NEW, dtype=jnp.int32)
        keys_all = jnp.concatenate([cached[:, :HD], keys_new[request]], axis=0).astype(jnp.float32)
        vals_all = jnp.concatenate([cached[:, HD:], values_new[request]], axis=0).astype(jnp.float32)
        seen_cached = (key_pos[None, :] >= 0) & (key_pos[None, :] > query_pos[:, None] - WIN)
        seen_new = jnp.arange(NEW)[None, :] <= jnp.arange(NEW)[:, None]
        visible = jnp.concatenate([seen_cached, seen_new], axis=1)[:, None, :]
        scores = jnp.einsum('thd,kd->thk', queries[request].astype(jnp.float32), keys_all) * scale
        peak = lax.optimization_barrier(jnp.max(jnp.where(visible, scores, -jnp.inf), axis=-1, keepdims=True))
        weights = jnp.where(visible, jnp.exp(scores - peak), 0.0)
        denominator = lax.optimization_barrier(jnp.sum(weights, axis=-1, keepdims=True))
        rounded = lax.optimization_barrier(weights.astype(jnp.bfloat16)).astype(jnp.float32)
        mixed = jnp.einsum('thk,kd->thd', rounded, vals_all) / denominator
        return mixed.reshape(NEW, H * HD)
    attended = lax.map(attend, jnp.arange(REQ, dtype=jnp.int32)).astype(jnp.bfloat16).reshape(REQ * NEW, H * HD)
    heads_out = jnp.dot(attended, out_weight.T, preferred_element_type=jnp.float32).astype(jnp.bfloat16)
    residual = (tokens.reshape(REQ * NEW, D).astype(jnp.float32) + heads_out.astype(jnp.float32)).astype(jnp.bfloat16)
    hidden_in = rms_norm(residual, mlp_gain).astype(jnp.bfloat16)
    gate = jnp.dot(hidden_in, gate_up[0].T, preferred_element_type=jnp.float32)
    upward = jnp.dot(hidden_in, gate_up[1].T, preferred_element_type=jnp.float32)
    hidden = (jax.nn.gelu(gate, approximate=True) * upward).astype(jnp.bfloat16)
    down_sum = jnp.dot(hidden, down_weight, preferred_element_type=jnp.float32)
    layer_out = (residual.astype(jnp.float32) + down_sum).astype(jnp.bfloat16).reshape(REQ, NEW, D)
    page_index = jnp.mod(positions_int // PAGE, NP).astype(jnp.int32)
    slot_taken = jnp.take_along_axis(page_table, page_index, axis=1)
    group_index = (jnp.arange(REQ, dtype=jnp.int32) // R_DEV)[:, None]
    target = group_index * group_slots + slot_taken
    offset = jnp.mod(positions_int, PAGE).astype(jnp.int32)
    written_pool = kv_pool.at[target, offset].set(jnp.concatenate([keys_new, values_new], axis=-1))
    return (layer_out, written_pool)
```

```python
import functools

import jax
import jax.numpy as jnp
import numpy as np
from jax import lax
from jax.experimental import pallas as pl
from jax.experimental.pallas import tpu as pltpu
from jax.sharding import PartitionSpec as P

MESH = pl.DeviceIdType.MESH
LOW = -1e30
F32 = jnp.float32
BF16 = jnp.bfloat16

D = 2560
H = 10
HD = 256
PAGE = 128
WIN = 2048
NEW = 4
R = 16
NP = 16
SLOTS = 16
NZ = 8
NS = 32
ROWS = R * NEW
FFL = 240
CB = 640
RHS_T = (((1,), (1,)), ((), ()))


def iota(shape, dim):
    return lax.broadcasted_iota(jnp.int32, shape, dim)


def layer_kernel(
    tok_ref, ag_ref, qkv_ref, ow_ref, mg_ref, gu_hbm, dn_hbm, kv_hbm, len_ref, pt_ref, inv_ref,
    out_ref, new_ref,
    tokf, normed, wq, wall, wo, pj, selq, selo, cosb, sinb, bias, biasn, kv, gu, dn,
    qs, kn, vn, sc, scn, mx, lx, acc, rs_s, rs_r, emat, att, ho, resid, r2_s, r2_r,
    load_sem, zs_sem, zr_sem, os_sem, or_sem, ph_send, ph_recv,
):
    z = lax.axis_index("dp")
    s = lax.axis_index("seq")

    loads = [
        pltpu.make_async_copy(kv_hbm, kv, load_sem.at[0]),
        pltpu.make_async_copy(gu_hbm, gu, load_sem.at[1]),
        pltpu.make_async_copy(dn_hbm, dn, load_sem.at[2]),
    ]
    for copy in loads:
        copy.start()

    barrier = pltpu.get_barrier_semaphore()

    def greet_seq(i, carry):
        pl.semaphore_signal(barrier, inc=1, device_id=(z, lax.rem(s + i, NS)), device_id_type=MESH)
        return carry

    def greet_dp(i, carry):
        pl.semaphore_signal(barrier, inc=1, device_id=(lax.rem(z + i, NZ), s), device_id_type=MESH)
        return carry

    lax.fori_loop(1, NZ, greet_dp, 0)
    lax.fori_loop(1, NS, greet_seq, 0)

    tokf[...] = tok_ref[...].astype(F32)
    for t in range(NEW):
        x = tokf[:, t, :]
        y = x * lax.rsqrt(jnp.mean(x * x, axis=-1, keepdims=True) + 1e-06) * ag_ref[...]
        normed[pl.ds(R * t, R), :] = y.astype(BF16)

    pl.semaphore_wait(barrier, NZ - 1 + NS - 1)

    up = lax.rem(z + 1, NZ)
    down = lax.rem(z + NZ - 1, NZ)
    half = D // 2

    def ring(direction, step, chunk):
        cols = pl.ds(chunk * half, half)
        if direction == 0:
            src = qkv_ref if step == 1 else wq.at[NZ - (step - 1)]
            dst, peer = wq.at[NZ - step], up
        else:
            src = qkv_ref if step == 1 else wq.at[step - 1]
            dst, peer = wq.at[step], down
        return pltpu.make_async_remote_copy(
            src_ref=src.at[:, cols],
            dst_ref=dst.at[:, cols],
            send_sem=zs_sem.at[direction, step - 1, chunk],
            recv_sem=zr_sem.at[direction, step - 1, chunk],
            device_id=(peer, s),
            device_id_type=MESH,
        )

    def carried(direction, step, chunk):
        return step < 4 or chunk == direction

    for chunk in range(2):
        for direction in range(2):
            ring(direction, 1, chunk).start()

    def pass_on(step):
        for chunk in range(2):
            for direction in range(2):
                if carried(direction, step, chunk):
                    ring(direction, step, chunk).wait_recv()
                    if step < 4 and carried(direction, step + 1, chunk):
                        ring(direction, step + 1, chunk).start()

    wall[...] = jnp.zeros_like(wall)
    wall[0, pl.ds(0, 12), :] = qkv_ref[...]

    lens = jnp.zeros((R, 1), jnp.int32)
    row_id = iota((R, 1), 0)
    for r in range(R):
        lens = jnp.where(row_id == r, len_ref[r], lens)
    for t in range(NEW):
        angle = (lens + t).astype(F32) * inv_ref[...]
        cosine = jnp.cos(angle)
        sine = jnp.sin(angle)
        sign = jnp.where(iota((R, 128), 1) < 64, -1.0, 1.0)
        cosb[pl.ds(R * t, R), :] = cosine
        sinb[pl.ds(R * t, R), :] = sine * sign

    pass_on(1)
    for c in range(4):
        rows = iota((128, 384), 0)
        part = rows % 16
        target = 96 * c + 12 * ((rows // 16 + z) % NZ) + part
        hit = (target == iota((128, 384), 1)) & (part < 12)
        selq[pl.ds(128 * c, 128), :] = jnp.where(hit, 1.0, 0.0).astype(BF16)
    wall[NZ - 1, pl.ds(0, 12), :] = wq[NZ - 1]
    wall[1, pl.ds(0, 12), :] = wq[1]
    pass_on(2)
    wall[NZ - 2, pl.ds(0, 12), :] = wq[NZ - 2]
    wall[2, pl.ds(0, 12), :] = wq[2]

    local = pt_ref[...] - s * SLOTS

    def mask_block(kb, carry):
        lane = iota((R, 256), 1)
        slot = kb * 2 + lane // PAGE
        page = jnp.full((R, 256), -1, jnp.int32)
        for i in range(NP):
            page = jnp.where(local[:, i : i + 1] == slot, i, page)
        last = lens - 1
        key_pos = last - ((last - (page * PAGE + lane % PAGE)) & (WIN - 1))
        fine = (page >= 0) & (key_pos >= 0)
        for t in range(NEW):
            seen = fine & (key_pos > lens + (t - WIN))
            bias[kb, pl.ds(R * t, R), :] = jnp.where(seen, 0.0, LOW)
        return carry

    lax.fori_loop(0, 8, mask_block, 0)
    key_id = iota((R, 128), 1)
    for t in range(NEW):
        seen = (key_id < ROWS) & (key_id % R == iota((R, 128), 0)) & (key_id // R <= t) & (s == 0)
        biasn[pl.ds(R * t, R), :] = jnp.where(seen, 0.0, LOW)

    pass_on(3)
    wall[NZ - 3, pl.ds(0, 12), :] = wq[NZ - 3]
    wall[3, pl.ds(0, 12), :] = wq[3]
    pass_on(4)
    wall[4, pl.ds(0, 12), :] = wq[4]

    def send_out(i):
        return pltpu.make_async_remote_copy(
            src_ref=ow_ref,
            dst_ref=wo.at[NZ - i],
            send_sem=os_sem,
            recv_sem=or_sem,
            device_id=(lax.rem(z + i, NZ), s),
            device_id_type=MESH,
        )

    def start_out(i, carry):
        send_out(i).start()
        return carry

    lax.fori_loop(1, NZ, start_out, 0)

    def gather_copy(phase, buf, i):
        return pltpu.make_async_remote_copy(
            src_ref=buf.at[s],
            dst_ref=buf.at[s],
            send_sem=ph_send.at[phase],
            recv_sem=ph_recv.at[phase],
            device_id=(z, lax.rem(s + i, NS)),
            device_id_type=MESH,
        )

    def scatter_copy(phase, src, dst, i):
        peer = lax.rem(s + i, NS)
        return pltpu.make_async_remote_copy(
            src_ref=src.at[peer],
            dst_ref=dst.at[s],
            send_sem=ph_send.at[phase],
            recv_sem=ph_recv.at[phase],
            device_id=(z, peer),
            device_id_type=MESH,
        )

    def start_all(make):
        def one(i, carry):
            make(i).start()
            return carry

        lax.fori_loop(1, NS, one, 0)

    def wait_bytes(ref, sem):
        pltpu.make_async_copy(ref, ref, sem).wait()

    def received(phase, buf):
        wait_bytes(buf.at[pl.ds(0, NS - 1)], ph_recv.at[phase])

    def sent(phase, buf):
        wait_bytes(buf.at[pl.ds(0, NS - 1)], ph_send.at[phase])

    part = lax.dot_general(
        normed[...], wall[...].reshape(128, D), RHS_T, preferred_element_type=F32
    )
    pj[s] = part.astype(BF16)
    start_all(functools.partial(gather_copy, 0, pj))
    for c in range(8):
        rows = iota((128, CB), 0)
        lanes = rows % 16
        target = 80 * c + 10 * ((rows // 16 + z) % NZ) + lanes
        hit = (target == iota((128, CB), 1)) & (lanes < 10)
        selo[pl.ds(128 * c, 128), :] = jnp.where(hit, 1.0, 0.0).astype(BF16)
    col_block = lax.rem(s, 4)
    lane = iota((128, CB), 0)
    head_of = (col_block * 5 + iota((128, CB), 1) // 128) // 2
    emat[...] = jnp.where((lane % 16 == head_of) & (lane < 48), 1.0, 0.0).astype(BF16)
    kn[...] = jnp.zeros_like(kn)
    vn[...] = jnp.zeros_like(vn)
    loads[0].wait()
    received(0, pj)

    groups = jnp.concatenate(
        [pj[...].reshape(8, 4, ROWS, 128)[:, c].reshape(8 * ROWS, 128) for c in range(4)], axis=1
    )
    proj = jnp.dot(groups, selq[...], preferred_element_type=F32)

    def unit(u):
        g, c = u // 3, u % 3
        return proj[ROWS * g : ROWS * (g + 1), 128 * c : 128 * (c + 1)]

    def turned(v):
        return v * cosb[...] + pltpu.roll(v, 64, 1) * sinb[...]

    for h in range(H):
        qs[pl.ds(ROWS * h, ROWS), pl.ds(0, 128)] = (
            turned(unit(2 * h)).astype(BF16) * jnp.asarray(HD ** -0.5, BF16)
        )
        qs[pl.ds(ROWS * h, ROWS), pl.ds(128, 128)] = (
            unit(2 * h + 1).astype(BF16) * jnp.asarray(HD ** -0.5, BF16)
        )
    kn[pl.ds(0, ROWS), pl.ds(0, 128)] = turned(unit(20)).astype(BF16)
    kn[pl.ds(0, ROWS), pl.ds(128, 128)] = unit(21).astype(BF16)
    vn[pl.ds(0, ROWS), pl.ds(0, 128)] = unit(22).astype(BF16)
    vn[pl.ds(0, ROWS), pl.ds(128, 128)] = unit(23).astype(BF16)
    new_ref[:, pl.ds(0, HD)] = kn[pl.ds(0, ROWS), :].astype(F32)
    new_ref[:, pl.ds(HD, HD)] = vn[pl.ds(0, ROWS), :].astype(F32)

    score_n = lax.dot_general(qs[...], kn[...], RHS_T, preferred_element_type=F32)
    score_n = (score_n.reshape(H, ROWS, 128) + biasn[...][None]).reshape(H * ROWS, 128)
    scn[...] = score_n
    mx[...] = score_n

    def score_block(kb, carry):
        keys = kv[pl.ds(kb * 2, 2), :, pl.ds(0, HD)].reshape(256, HD)
        value = lax.dot_general(qs[...], keys, RHS_T, preferred_element_type=F32)
        value = (value.reshape(H, ROWS, 256) + bias[kb][None]).reshape(H * ROWS, 256)
        sc[kb] = value
        mx[...] = jnp.maximum(mx[...], jnp.maximum(value[:, :128], value[:, 128:]))
        return carry

    lax.fori_loop(0, 8, score_block, 0)
    peak = jnp.max(mx[...], axis=1, keepdims=True)
    mx[...] = jnp.broadcast_to(peak, mx.shape)
    weight = jnp.exp(scn[...] - mx[...])
    lx[...] = weight
    acc[...] = jnp.dot(weight.astype(BF16), vn[...], preferred_element_type=F32)

    def value_block(kb, carry):
        left = jnp.exp(sc[kb, :, pl.ds(0, 128)] - mx[...])
        right = jnp.exp(sc[kb, :, pl.ds(128, 128)] - mx[...])
        lx[...] += left + right
        both = jnp.concatenate([left.astype(BF16), right.astype(BF16)], axis=1)
        values = kv[pl.ds(kb * 2, 2), :, pl.ds(HD, HD)].reshape(256, HD)
        acc[...] += jnp.dot(both, values, preferred_element_type=F32)
        return carry

    lax.fori_loop(0, 8, value_block, 0)
    total = jnp.sum(lx[...], axis=1, keepdims=True)
    level = mx[...] + jnp.log(jnp.broadcast_to(total, mx.shape))
    mixed = acc[...] / total
    lane_h = iota((ROWS, 128), 1)
    table = jnp.zeros((ROWS, 128), F32)
    for h in range(H):
        table = jnp.where(lane_h % 16 == h, level[ROWS * h : ROWS * (h + 1)], table)
        for side in range(2):
            u = 2 * h + side
            piece = mixed[ROWS * h : ROWS * (h + 1), 128 * side : 128 * (side + 1)]
            rs_s[:, u // 5, :, pl.ds(128 * (u % 5), 128)] = piece.reshape(8, 8, 128).astype(BF16)
    first = table.astype(BF16).astype(F32)
    second = (table - first).astype(BF16).astype(F32)
    third = table - first - second
    table = jnp.where(lane_h < 16, first, jnp.where(lane_h < 32, second, third))
    table = jnp.where(lane_h % 16 < H, table, 0.0).reshape(8, 8, 128).astype(BF16)
    for c in range(4):
        rs_s[:, c, :, pl.ds(CB, 128)] = table

    def flat(ref):
        return ref

    def part_copy(i):
        peer = lax.rem(s + i, NS)
        return pltpu.make_async_remote_copy(
            src_ref=rs_s.at[peer // 4, peer % 4],
            dst_ref=rs_r.at[s],
            send_sem=ph_send.at[1],
            recv_sem=ph_recv.at[1],
            device_id=(z, peer),
            device_id_type=MESH,
        )

    start_all(part_copy)
    rs_r[s] = rs_s[s // 4, s % 4]
    received(1, rs_r)
    levels = rs_r[:, :, pl.ds(CB, 128)].astype(F32).reshape(NS * 8, 128).astype(BF16)
    levels = jnp.dot(levels, emat[...], preferred_element_type=F32).reshape(NS, 8, CB)
    factor = jnp.exp(levels - jnp.max(levels, axis=0, keepdims=True))
    number = jnp.sum(factor * rs_r[:, :, pl.ds(0, CB)].astype(F32), axis=0)
    attended = number / jnp.sum(factor, axis=0)

    att[s] = attended.astype(BF16)
    start_all(functools.partial(gather_copy, 2, att))
    wait_bytes(wo.at[pl.ds(1, NZ - 1)], or_sem)
    wall[...] = jnp.zeros_like(wall)
    wall[0, pl.ds(0, 10), :] = ow_ref[...]
    for d in range(1, NZ):
        wall[d, pl.ds(0, 10), :] = wo[d]
    received(2, att)
    rows_att = att[...].astype(F32).reshape(8, 4, 8, CB)
    part = jnp.zeros((ROWS, 128), F32)
    for c in range(4):
        left = rows_att[:, c].reshape(ROWS, CB).astype(BF16)
        part += lax.dot_general(
            left, wall[:, :, pl.ds(CB * c, CB)].reshape(128, CB), RHS_T, preferred_element_type=F32
        )

    ho[s] = part.astype(BF16)
    start_all(functools.partial(gather_copy, 3, ho))
    loads[1].wait()
    loads[2].wait()
    received(3, ho)
    groups = jnp.concatenate(
        [ho[...].reshape(4, 8, ROWS, 128)[:, c].reshape(4 * ROWS, 128) for c in range(8)], axis=1
    )
    heads_out = jnp.dot(groups, selo[...], preferred_element_type=F32)
    square = jnp.zeros((ROWS, 1), F32)
    pieces = []
    for c in range(4):
        cols = pl.ds(CB * c, CB)
        x = jnp.concatenate([tokf[:, t, cols] for t in range(NEW)], axis=0)
        x = (x + heads_out[ROWS * c : ROWS * (c + 1)]).astype(BF16).astype(F32)
        pieces.append(x)
        resid[:, c] = x.reshape(8, 8, CB)
        square += jnp.sum(x * x, axis=1, keepdims=True)
    scale = lax.rsqrt(square * (1.0 / D) + 1e-06)
    gate = jnp.zeros((ROWS, FFL), F32)
    lift = jnp.zeros((ROWS, FFL), F32)
    for c in range(4):
        cols = pl.ds(CB * c, CB)
        entry = (pieces[c] * scale * mg_ref[:, cols]).astype(BF16)
        gate += lax.dot_general(entry, gu[0, :, cols], RHS_T, preferred_element_type=F32)
        lift += lax.dot_general(entry, gu[1, :, cols], RHS_T, preferred_element_type=F32)
    inner = np.float32(np.sqrt(2.0 / np.pi)) * (gate + 0.044715 * (gate * gate * gate))
    hidden = (0.5 * gate * (1.0 + jnp.tanh(inner)) * lift).astype(BF16)
    for c in range(4):
        value = jnp.dot(hidden, dn[:, pl.ds(CB * c, CB)], preferred_element_type=F32)
        r2_s[:, c] = value.reshape(8, 8, CB).astype(BF16)

    def sum_copy(i):
        peer = lax.rem(s + i, NS)
        return pltpu.make_async_remote_copy(
            src_ref=r2_s.at[peer // 4, peer % 4],
            dst_ref=r2_r.at[s],
            send_sem=ph_send.at[4],
            recv_sem=ph_recv.at[4],
            device_id=(z, peer),
            device_id_type=MESH,
        )

    start_all(sum_copy)
    r2_r[s] = r2_s[s // 4, s % 4]
    received(4, r2_r)
    done = jnp.sum(r2_r[...].astype(F32), axis=0) + resid[s // 4, s % 4]

    out_ref[s] = done.astype(BF16)
    start_all(functools.partial(gather_copy, 5, out_ref))
    for direction in range(2):
        for step in range(1, 5):
            for chunk in range(2):
                if carried(direction, step, chunk):
                    ring(direction, step, chunk).wait_send()
    wait_bytes(wo.at[pl.ds(1, NZ - 1)], os_sem)
    sent(0, pj)
    sent(1, rs_r)
    sent(2, att)
    sent(3, ho)
    sent(4, r2_r)
    received(5, out_ref)
    sent(5, out_ref)


def write_kernel(s_ref, len_ref, pt_ref, kv_hbm, new_ref, out_hbm, pool, in_sem, out_sem):
    s = s_ref[0]
    copies = [pltpu.make_async_copy(kv_hbm.at[p], pool.at[p], in_sem.at[p]) for p in range(SLOTS)]
    for copy in copies:
        copy.start()
    for copy in copies:
        copy.wait()

    def one(n, carry):
        r = n // NEW
        t = n % NEW
        pos = len_ref[r] + t
        slot = pt_ref[r, (pos // PAGE) % NP] - s * SLOTS

        @pl.when((slot >= 0) & (slot < SLOTS))
        def _():
            place = pos % PAGE
            base = pl.multiple_of((place // 16) * 16, 16)
            old = pool[slot, pl.ds(base, 16), :].astype(F32)
            row = new_ref[pl.ds(t * R + r, 1), :]
            mixed = jnp.where(iota((16, 2 * HD), 0) == place - base, row, old)
            pool[slot, pl.ds(base, 16), :] = mixed.astype(BF16)

        return carry

    lax.fori_loop(0, ROWS, one, 0)
    copies = [pltpu.make_async_copy(pool.at[p], out_hbm.at[p], out_sem.at[p]) for p in range(SLOTS)]
    for copy in copies:
        copy.start()
    for copy in copies:
        copy.wait()


def body(
    tokens,
    attn_gain,
    qkv_weight,
    out_weight,
    mlp_gain,
    gate_up,
    down_weight,
    kv_pool,
    cache_len,
    page_table,
):
    freq = np.arange(64, dtype=np.float64)
    inverse = (10000.0 ** (-freq / 64)).astype(np.float32)
    inverse = jnp.asarray(np.concatenate([inverse, inverse])[None, :])
    vmem = pl.BlockSpec(memory_space=pltpu.VMEM)
    smem = pl.BlockSpec(memory_space=pltpu.SMEM)
    hbm = pl.BlockSpec(memory_space=pl.ANY)
    dma = pltpu.SemaphoreType.DMA
    blocks, new_rows = pl.pallas_call(
        layer_kernel,
        out_shape=(
            jax.ShapeDtypeStruct((NS, 8, CB), BF16),
            jax.ShapeDtypeStruct((ROWS, 2 * HD), F32),
        ),
        in_specs=[vmem] * 5 + [hbm] * 3 + [smem, vmem, vmem],
        out_specs=(vmem, vmem),
        scratch_shapes=[
            pltpu.VMEM((R, NEW, D), F32),
            pltpu.VMEM((ROWS, D), BF16),
            pltpu.VMEM((NZ, 12, D), BF16),
            pltpu.VMEM((NZ, 16, D), BF16),
            pltpu.VMEM((NZ, 10, D), BF16),
            pltpu.VMEM((NS, ROWS, 128), BF16),
            pltpu.VMEM((512, 384), BF16),
            pltpu.VMEM((1024, CB), BF16),
            pltpu.VMEM((ROWS, 128), F32),
            pltpu.VMEM((ROWS, 128), F32),
            pltpu.VMEM((8, ROWS, 256), F32),
            pltpu.VMEM((ROWS, 128), F32),
            pltpu.VMEM((SLOTS, PAGE, 2 * HD), BF16),
            pltpu.VMEM((2, FFL, D), BF16),
            pltpu.VMEM((FFL, D), BF16),
            pltpu.VMEM((H * ROWS, HD), BF16),
            pltpu.VMEM((128, HD), BF16),
            pltpu.VMEM((128, HD), BF16),
            pltpu.VMEM((8, H * ROWS, 256), F32),
            pltpu.VMEM((H * ROWS, 128), F32),
            pltpu.VMEM((H * ROWS, 128), F32),
            pltpu.VMEM((H * ROWS, 128), F32),
            pltpu.VMEM((H * ROWS, HD), F32),
            pltpu.VMEM((8, 4, 8, CB + 128), BF16),
            pltpu.VMEM((NS, 8, CB + 128), BF16),
            pltpu.VMEM((128, CB), BF16),
            pltpu.VMEM((NS, 8, CB), BF16),
            pltpu.VMEM((NS, ROWS, 128), BF16),
            pltpu.VMEM((8, 4, 8, CB), F32),
            pltpu.VMEM((8, 4, 8, CB), BF16),
            pltpu.VMEM((NS, 8, CB), BF16),
            dma((3,)),
            dma((2, 4, 2)),
            dma((2, 4, 2)),
            dma(()),
            dma(()),
            dma((6,)),
            dma((6,)),
        ],
        compiler_params=pltpu.CompilerParams(
            collective_id=0, has_side_effects=True, vmem_limit_bytes=60 * 1024 * 1024
        ),
        name="layer",
    )(
        tokens,
        attn_gain.reshape(1, D),
        qkv_weight,
        out_weight,
        mlp_gain.reshape(1, D),
        gate_up,
        down_weight,
        kv_pool,
        cache_len,
        page_table,
        inverse,
    )
    written_pool = pl.pallas_call(
        write_kernel,
        out_shape=jax.ShapeDtypeStruct((SLOTS, PAGE, 2 * HD), BF16),
        in_specs=[smem, smem, smem, hbm, vmem],
        out_specs=hbm,
        scratch_shapes=[pltpu.VMEM((SLOTS, PAGE, 2 * HD), BF16), dma((SLOTS,)), dma((SLOTS,))],
        name="write",
    )(lax.axis_index("seq").reshape(1), cache_len, page_table, kv_pool, new_rows)
    layer_out = blocks.reshape(4, 2, 4, 8, CB).transpose(1, 3, 0, 2, 4).reshape(R, NEW, D)
    return (layer_out, written_pool)


def solution(mesh):
    in_specs = (
        P("dp", None, None),
        P(),
        P(("seq", "dp"), None),
        P(("seq", "dp"), None),
        P(),
        P(None, "seq", None),
        P("seq", None),
        P(("dp", "seq"), None, None),
        P("dp"),
        P("dp", None),
    )
    out_specs = (P("dp", None, None), P(("dp", "seq"), None, None))
    return jax.shard_map(body, mesh=mesh, in_specs=in_specs, out_specs=out_specs, check_vma=False)
```

```python
import functools

import jax
import jax.numpy as jnp
import numpy as np
from jax import lax
from jax.experimental import pallas as pl
from jax.experimental.pallas import tpu as pltpu
from jax.sharding import PartitionSpec as P

MESH = pl.DeviceIdType.MESH
LOW = -1e30
F32 = jnp.float32
BF16 = jnp.bfloat16

D = 2560
H = 10
HD = 256
PAGE = 128
WIN = 2048
NEW = 4
R = 16
NP = 16
SLOTS = 16
NZ = 8
NS = 32
ROWS = R * NEW
FFL = 240
CB = 640
RHS_T = (((1,), (1,)), ((), ()))


def iota(shape, dim):
    return lax.broadcasted_iota(jnp.int32, shape, dim)


OFFSETS = sorted(
    [(dx, dy) for dx in range(4) for dy in range(4) if dx + dy > 0],
    key=lambda o: min(o[0], 4 - o[0]) + min(o[1], 4 - o[1]),
)


def layer_kernel(
    tok_ref, ag_ref, qkv_ref, ow_ref, mg_ref, gu_hbm, dn_hbm, kv_hbm, len_ref, pt_ref, inv_ref,
    out_ref, pool_ref,
    tokf, tokr, normed, wq, wall, wo, pj, selq, selo, cosb, sinb, bias, biasn, place, kv, gu, dn,
    qs, kn, vn, fresh, sc, scn, mx, lx, acc, rs_s, rs_r, emat, att, ho, resid, r2_s, r2_r,
    load_sem, zs_sem, zr_sem, os_sem, or_sem, ph_send, ph_recv, near_recv, pair_recv,
):
    z = lax.axis_index("dp")
    s = lax.axis_index("seq")
    chip, core = s // 2, lax.rem(s, 2)
    chip_x, chip_y = chip // 4, lax.rem(chip, 4)

    loads = [
        pltpu.make_async_copy(kv_hbm, kv, load_sem.at[0]),
        pltpu.make_async_copy(gu_hbm, gu, load_sem.at[1]),
        pltpu.make_async_copy(dn_hbm, dn, load_sem.at[2]),
    ]
    barrier = pltpu.get_barrier_semaphore()

    def greet_seq(i, carry):
        pl.semaphore_signal(barrier, inc=1, device_id=(z, lax.rem(s + i, NS)), device_id_type=MESH)
        return carry

    def greet_dp(i, carry):
        pl.semaphore_signal(barrier, inc=1, device_id=(lax.rem(z + i, NZ), s), device_id_type=MESH)
        return carry

    lax.fori_loop(1, NZ, greet_dp, 0)
    lax.fori_loop(1, NS, greet_seq, 0)
    for copy in loads:
        copy.start()

    def gains(ref):
        return jnp.concatenate([ref[i : i + 1, :] for i in range(D // 128)], axis=1)

    tokf[...] = tok_ref[...].astype(F32)
    by_token = jnp.concatenate([tokf[:, t, :] for t in range(NEW)], axis=0).astype(BF16)
    rows, cols = iota((ROWS, ROWS), 0), iota((ROWS, ROWS), 1)
    order = (cols // R == rows % NEW) & (cols % R == rows // NEW)
    tokr[...] = jnp.dot(
        jnp.where(order, 1.0, 0.0).astype(BF16), by_token, preferred_element_type=F32
    )
    gain = gains(ag_ref)
    for b in range(4):
        x = tokr[pl.ds(16 * b, 16), :]
        y = x * lax.rsqrt(jnp.mean(x * x, axis=-1, keepdims=True) + 1e-06) * gain
        normed[pl.ds(16 * b, 16), :] = y.astype(BF16)

    row_id = iota((ROWS, 1), 0)
    lens = jnp.zeros((ROWS, 1), jnp.int32)
    table_pages = jnp.zeros((ROWS, NP), jnp.int32)
    for r in range(R):
        mine = row_id // NEW == r
        lens = jnp.where(mine, len_ref[r], lens)
        table_pages = jnp.where(mine, pt_ref[r : r + 1, :], table_pages)
    token = row_id % NEW
    pos = lens + token

    pl.semaphore_wait(barrier, NZ - 1 + NS - 1)

    half = D // 2

    def hop(src, buf, sems, sign, away, chunk):
        send, recv = sems
        own = away <= 2
        came = NZ - 2 if sign > 0 else 2
        dist = away if own else away - 2
        slot = NZ - away if sign > 0 else away
        cols = pl.ds(chunk * half, half)
        side = 0 if sign > 0 else 1
        ref = src if own else buf.at[came]
        return pltpu.make_async_remote_copy(
            src_ref=ref.at[:, cols],
            dst_ref=buf.at[slot].at[:, cols],
            send_sem=send.at[side, away - 1, chunk],
            recv_sem=recv.at[side, away - 1, chunk],
            device_id=(lax.rem(z + NZ + sign * dist, NZ), s),
            device_id_type=MESH,
        )

    def chunks(sign, away):
        return (0, 1) if away < 4 else ((0,) if sign > 0 else (1,))

    q_hop = functools.partial(hop, qkv_ref, wq, (zs_sem, zr_sem))
    o_hop = functools.partial(hop, ow_ref, wo, (os_sem, or_sem))

    def send_own(move):
        for away in (2, 1):
            for i in range(2):
                for sign in (1, -1):
                    chunk = i if sign > 0 else 1 - i
                    move(sign, away, chunk).start()

    def send_on(move):
        for i in range(2):
            for sign in (1, -1):
                chunk = i if sign > 0 else 1 - i
                move(sign, 2, chunk).wait_recv()
                for away in (4, 3):
                    if chunk in chunks(sign, away):
                        move(sign, away, chunk).start()

    def arrived(move, away):
        for sign in (1, -1):
            for chunk in chunks(sign, away):
                move(sign, away, chunk).wait_recv()

    def left(move):
        for away in range(1, 5):
            for sign in (1, -1):
                for chunk in chunks(sign, away):
                    move(sign, away, chunk).wait_send()

    send_own(q_hop)

    angle = pos.astype(F32) * inv_ref[...]
    cosb[...] = jnp.cos(angle)
    sinb[...] = jnp.sin(angle) * jnp.where(iota((ROWS, 128), 1) < 64, -1.0, 1.0)
    wall[...] = jnp.zeros_like(wall)
    wall[0, pl.ds(0, 12), :] = qkv_ref[...]

    send_on(q_hop)

    for c in range(4):
        rows = iota((128, 384), 0)
        part = rows % 16
        target = 96 * c + 12 * ((rows // 16 + z) % NZ) + part
        hit = (target == iota((128, 384), 1)) & (part < 12)
        selq[pl.ds(128 * c, 128), :] = jnp.where(hit, 1.0, 0.0).astype(BF16)
    arrived(q_hop, 1)
    for d in (1, 2, 6, 7):
        wall[d, pl.ds(0, 12), :] = wq[d]

    local = table_pages - s * SLOTS

    def mask_block(kb, carry):
        lane = iota((ROWS, 256), 1)
        slot = kb * 2 + lane // PAGE
        page = jnp.full((ROWS, 256), -1, jnp.int32)
        for i in range(NP):
            page = jnp.where(local[:, i : i + 1] == slot, i, page)
        last = lens - 1
        cycle = page * PAGE + lane % PAGE
        key_pos = last - ((last - cycle) & (WIN - 1))
        seen = (page >= 0) & (key_pos >= 0) & (key_pos > pos - WIN)
        bias[kb] = jnp.where(seen, 0.0, LOW)
        place[kb] = jnp.where(cycle == (pos & (WIN - 1)), 1.0, 0.0).astype(BF16)
        return carry

    lax.fori_loop(0, 8, mask_block, 0)
    key_id = iota((ROWS, 128), 1)
    seen = (key_id // NEW == row_id // NEW) & (key_id % NEW <= token) & (s == 0)
    biasn[...] = jnp.where(seen, 0.0, LOW)

    arrived(q_hop, 3)
    arrived(q_hop, 4)
    for d in (3, 4, 5):
        wall[d, pl.ds(0, 12), :] = wq[d]

    def wait_bytes(ref, sem):
        pltpu.make_async_copy(ref, ref, sem).wait()

    def chip_at(dx, dy):
        return lax.rem(chip_x + dx, 4) * 4 + lax.rem(chip_y + dy, 4)

    def gather_start(phase, view):
        mine = view(chip, core)
        for j in reversed(range(15)):
            pltpu.make_async_remote_copy(
                src_ref=mine,
                dst_ref=mine,
                send_sem=ph_send.at[phase],
                recv_sem=near_recv.at[phase, j],
                device_id=(z, chip_at(*OFFSETS[j]) * 2 + core),
                device_id_type=MESH,
            ).start()
        to_pair(phase, mine)

    def to_pair(phase, ref):
        pltpu.make_async_remote_copy(
            src_ref=ref,
            dst_ref=ref,
            send_sem=ph_send.at[phase],
            recv_sem=pair_recv.at[phase],
            device_id=(z, chip * 2 + 1 - core),
            device_id_type=MESH,
        ).start()

    def gather_finish(phase, view, sixteen):
        for j in range(15):
            dx, dy = OFFSETS[j]
            ref = view(chip_at(4 - dx, 4 - dy), core)
            wait_bytes(ref, near_recv.at[phase, j])
            to_pair(phase, ref)
        wait_bytes(sixteen, pair_recv.at[phase])

    def gather_left(phase, sixteen, fifteen):
        wait_bytes(sixteen, ph_send.at[phase])
        wait_bytes(fifteen, ph_send.at[phase])

    def scatter_start(phase, src, dst):
        def one(peer):
            pltpu.make_async_remote_copy(
                src_ref=src.at[peer // 4, lax.rem(peer, 4)],
                dst_ref=dst.at[s],
                send_sem=ph_send.at[phase],
                recv_sem=ph_recv.at[phase],
                device_id=(z, peer),
                device_id_type=MESH,
            ).start()

        for j in reversed(range(15)):
            base = chip_at(*OFFSETS[j]) * 2
            one(base + core)
            one(base + 1 - core)
        one(chip * 2 + 1 - core)

    def scatter_wait(sem, phase, dst):
        wait_bytes(dst.at[pl.ds(0, NS - 1)], sem.at[phase])

    part = lax.dot_general(
        normed[...], wall[...].reshape(128, D), RHS_T, preferred_element_type=F32
    )
    pj_view = lambda where, which: pj.at[which, where]
    pj[core, chip] = part.astype(BF16)
    gather_start(0, pj_view)
    send_own(o_hop)
    for c in range(8):
        rows = iota((128, CB), 0)
        lanes = rows % 16
        target = 80 * c + 10 * ((rows // 16 + z) % NZ) + lanes
        hit = (target == iota((128, CB), 1)) & (lanes < 10)
        selo[pl.ds(128 * c, 128), :] = jnp.where(hit, 1.0, 0.0).astype(BF16)
    col_block = lax.rem(s, 4)
    lane = iota((128, CB), 0)
    head_of = (col_block * 5 + iota((128, CB), 1) // 128) // 2
    emat[...] = jnp.where((lane % 16 == head_of) & (lane < 48), 1.0, 0.0).astype(BF16)
    kn[...] = jnp.zeros_like(kn)
    vn[...] = jnp.zeros_like(vn)
    loads[0].wait()
    gather_finish(0, pj_view, pj.at[0])

    groups = jnp.concatenate(
        [
            pj[c % 2].reshape(8, 2, ROWS, 128)[:, c // 2].reshape(8 * ROWS, 128)
            for c in range(4)
        ],
        axis=1,
    )
    proj = jnp.dot(groups, selq[...], preferred_element_type=F32)

    def unit(u):
        g, c = u // 3, u % 3
        return proj[ROWS * g : ROWS * (g + 1), 128 * c : 128 * (c + 1)]

    def turned(v):
        return v * cosb[...] + pltpu.roll(v, 64, 1) * sinb[...]

    for h in range(H):
        qs[pl.ds(ROWS * h, ROWS), pl.ds(0, 128)] = (
            turned(unit(2 * h)).astype(BF16) * jnp.asarray(HD ** -0.5, BF16)
        )
        qs[pl.ds(ROWS * h, ROWS), pl.ds(128, 128)] = (
            unit(2 * h + 1).astype(BF16) * jnp.asarray(HD ** -0.5, BF16)
        )
    kn[pl.ds(0, ROWS), pl.ds(0, 128)] = turned(unit(20)).astype(BF16)
    kn[pl.ds(0, ROWS), pl.ds(128, 128)] = unit(21).astype(BF16)
    vn[pl.ds(0, ROWS), pl.ds(0, 128)] = unit(22).astype(BF16)
    vn[pl.ds(0, ROWS), pl.ds(128, 128)] = unit(23).astype(BF16)
    fresh[:, pl.ds(0, HD)] = kn[pl.ds(0, ROWS), :]
    fresh[:, pl.ds(HD, HD)] = vn[pl.ds(0, ROWS), :]

    send_on(o_hop)

    score_n = lax.dot_general(qs[...], kn[...], RHS_T, preferred_element_type=F32)
    score_n = (score_n.reshape(H, ROWS, 128) + biasn[...][None]).reshape(H * ROWS, 128)
    scn[...] = score_n
    mx[...] = score_n

    def score_block(kb, carry):
        keys = kv[pl.ds(kb * 2, 2), :, pl.ds(0, HD)].reshape(256, HD)
        value = lax.dot_general(qs[...], keys, RHS_T, preferred_element_type=F32)
        value = (value.reshape(H, ROWS, 256) + bias[kb][None]).reshape(H * ROWS, 256)
        sc[kb] = value
        mx[...] = jnp.maximum(mx[...], jnp.maximum(value[:, :128], value[:, 128:]))
        return carry

    lax.fori_loop(0, 8, score_block, 0)
    peak = jnp.max(mx[...], axis=1, keepdims=True)
    mx[...] = jnp.broadcast_to(peak, mx.shape)
    weight = jnp.exp(scn[...] - mx[...])
    lx[...] = weight
    acc[...] = jnp.dot(weight.astype(BF16), vn[...], preferred_element_type=F32)

    def value_block(kb, carry):
        left = jnp.exp(sc[kb, :, pl.ds(0, 128)] - mx[...])
        right = jnp.exp(sc[kb, :, pl.ds(128, 128)] - mx[...])
        lx[...] += left + right
        both = jnp.concatenate([left.astype(BF16), right.astype(BF16)], axis=1)
        values = kv[pl.ds(kb * 2, 2), :, pl.ds(HD, HD)].reshape(256, HD)
        acc[...] += jnp.dot(both, values, preferred_element_type=F32)
        return carry

    lax.fori_loop(0, 8, value_block, 0)
    total = jnp.sum(lx[...], axis=1, keepdims=True)
    level = mx[...] + jnp.log(jnp.broadcast_to(total, mx.shape))
    mixed = acc[...] / total
    lane_h = iota((ROWS, 128), 1)
    table = jnp.zeros((ROWS, 128), F32)
    for h in range(H):
        table = jnp.where(lane_h % 16 == h, level[ROWS * h : ROWS * (h + 1)], table)
        for side in range(2):
            u = 2 * h + side
            piece = mixed[ROWS * h : ROWS * (h + 1), 128 * side : 128 * (side + 1)]
            rs_s[:, u // 5, :, pl.ds(128 * (u % 5), 128)] = piece.reshape(8, 8, 128).astype(BF16)
    first = table.astype(BF16).astype(F32)
    second = (table - first).astype(BF16).astype(F32)
    third = table - first - second
    table = jnp.where(lane_h < 16, first, jnp.where(lane_h < 32, second, third))
    table = jnp.where(lane_h % 16 < H, table, 0.0).reshape(8, 8, 128).astype(BF16)
    for c in range(4):
        rs_s[:, c, :, pl.ds(CB, 128)] = table

    scatter_start(1, rs_s, rs_r)
    rs_r[s] = rs_s[s // 4, lax.rem(s, 4)]

    def write_block(kb, carry):
        news = lax.dot_general(place[kb], fresh[...], (((0,), (0,)), ((), ())), preferred_element_type=F32)
        ones = jnp.ones((ROWS, 2 * HD), BF16)
        hits = lax.dot_general(place[kb], ones, (((0,), (0,)), ((), ())), preferred_element_type=F32)
        olds = kv[pl.ds(kb * 2, 2)].reshape(2 * PAGE, 2 * HD).astype(F32)
        value = jnp.where(hits > 0.5, news, olds).astype(BF16)
        pool_ref[pl.ds(kb * 2, 2)] = value.reshape(2, PAGE, 2 * HD)
        return carry

    lax.fori_loop(0, 8, write_block, 0)
    wall[...] = jnp.zeros_like(wall)
    wall[0, pl.ds(0, 10), :] = ow_ref[...]
    for away in (1, 3, 4):
        arrived(o_hop, away)
    for d in range(1, NZ):
        wall[d, pl.ds(0, 10), :] = wo[d]
    scatter_wait(ph_recv, 1, rs_r)
    levels = rs_r[:, :, pl.ds(CB, 128)].astype(F32).reshape(NS * 8, 128).astype(BF16)
    levels = jnp.dot(levels, emat[...], preferred_element_type=F32).reshape(NS, 8, CB)
    factor = jnp.exp(levels - jnp.max(levels, axis=0, keepdims=True))
    number = jnp.sum(factor * rs_r[:, :, pl.ds(0, CB)].astype(F32), axis=0)
    attended = number / jnp.sum(factor, axis=0)

    att_view = lambda where, which: att.at[which, where]
    att[core, chip] = attended.astype(BF16)
    gather_start(2, att_view)
    gather_finish(2, att_view, att.at[0])
    part = jnp.zeros((ROWS, 128), F32)
    for c in range(4):
        left_rows = att[c % 2].astype(F32).reshape(8, 2, 8, CB)[:, c // 2].reshape(ROWS, CB)
        part += lax.dot_general(
            left_rows.astype(BF16), wall[:, :, pl.ds(CB * c, CB)].reshape(128, CB), RHS_T,
            preferred_element_type=F32,
        )

    ho_view = lambda where, which: ho.at[which, where]
    ho[core, chip] = part.astype(BF16)
    gather_start(3, ho_view)
    loads[1].wait()
    loads[2].wait()
    gain = gains(mg_ref)
    gather_finish(3, ho_view, ho.at[0])
    groups = jnp.concatenate(
        [
            ho[c % 2].reshape(4, 4, ROWS, 128)[:, c // 2].reshape(4 * ROWS, 128)
            for c in range(8)
        ],
        axis=1,
    )
    heads_out = jnp.dot(groups, selo[...], preferred_element_type=F32)
    square = jnp.zeros((ROWS, 1), F32)
    pieces = []
    for c in range(4):
        x = tokr[:, pl.ds(CB * c, CB)]
        x = (x + heads_out[ROWS * c : ROWS * (c + 1)]).astype(BF16).astype(F32)
        pieces.append(x)
        resid[:, c] = x.reshape(8, 8, CB)
        square += jnp.sum(x * x, axis=1, keepdims=True)
    scale = lax.rsqrt(square * (1.0 / D) + 1e-06)
    gate = jnp.zeros((ROWS, FFL), F32)
    lift = jnp.zeros((ROWS, FFL), F32)
    for c in range(4):
        cols = pl.ds(CB * c, CB)
        entry = (pieces[c] * scale * gain[:, CB * c : CB * (c + 1)]).astype(BF16)
        gate += lax.dot_general(entry, gu[0, :, cols], RHS_T, preferred_element_type=F32)
        lift += lax.dot_general(entry, gu[1, :, cols], RHS_T, preferred_element_type=F32)
    inner = np.float32(np.sqrt(2.0 / np.pi)) * (gate + 0.044715 * (gate * gate * gate))
    hidden = (0.5 * gate * (1.0 + jnp.tanh(inner)) * lift).astype(BF16)
    for c in range(4):
        value = jnp.dot(hidden, dn[:, pl.ds(CB * c, CB)], preferred_element_type=F32)
        r2_s[:, c] = value.reshape(8, 8, CB).astype(BF16)

    scatter_start(4, r2_s, r2_r)
    r2_r[s] = r2_s[s // 4, lax.rem(s, 4)]
    scatter_wait(ph_recv, 4, r2_r)
    done = jnp.sum(r2_r[...].astype(F32), axis=0) + resid[s // 4, lax.rem(s, 4)]

    def out_view(where, which):
        index = where * 2 + which
        cols = pl.ds(pl.multiple_of(lax.rem(index, 4) * CB, 128), CB)
        return out_ref.at[index // 4, :, cols]

    out_ref[s // 4, :, pl.ds(pl.multiple_of(lax.rem(s, 4) * CB, 128), CB)] = done.astype(BF16)
    gather_start(5, out_view)
    left(q_hop)
    left(o_hop)
    gather_left(0, pj.at[0], pj.at[0, pl.ds(0, 15)])
    gather_left(2, att.at[0], att.at[0, pl.ds(0, 15)])
    gather_left(3, ho.at[0], ho.at[0, pl.ds(0, 15)])
    scatter_wait(ph_send, 1, rs_r)
    scatter_wait(ph_send, 4, r2_r)
    gather_finish(5, out_view, att.at[0])
    gather_left(5, att.at[0], att.at[0, pl.ds(0, 15)])


def body(
    tokens,
    attn_gain,
    qkv_weight,
    out_weight,
    mlp_gain,
    gate_up,
    down_weight,
    kv_pool,
    cache_len,
    page_table,
):
    freq = np.arange(64, dtype=np.float64)
    inverse = (10000.0 ** (-freq / 64)).astype(np.float32)
    inverse = jnp.asarray(np.concatenate([inverse, inverse])[None, :])
    vmem = pl.BlockSpec(memory_space=pltpu.VMEM)
    smem = pl.BlockSpec(memory_space=pltpu.SMEM)
    hbm = pl.BlockSpec(memory_space=pltpu.HBM)
    dma = pltpu.SemaphoreType.DMA
    blocks, written_pool = pl.pallas_call(
        layer_kernel,
        out_shape=(
            jax.ShapeDtypeStruct((8, 8, D), BF16),
            jax.ShapeDtypeStruct((SLOTS, PAGE, 2 * HD), BF16),
        ),
        in_specs=[vmem] * 5 + [hbm] * 3 + [smem, vmem, vmem],
        out_specs=(vmem, vmem),
        scratch_shapes=[
            pltpu.VMEM((R, NEW, D), F32),
            pltpu.VMEM((ROWS, D), F32),
            pltpu.VMEM((ROWS, D), BF16),
            pltpu.VMEM((NZ, 12, D), BF16),
            pltpu.VMEM((NZ, 16, D), BF16),
            pltpu.VMEM((NZ, 10, D), BF16),
            pltpu.VMEM((2, 16, ROWS, 128), BF16),
            pltpu.VMEM((512, 384), BF16),
            pltpu.VMEM((1024, CB), BF16),
            pltpu.VMEM((ROWS, 128), F32),
            pltpu.VMEM((ROWS, 128), F32),
            pltpu.VMEM((8, ROWS, 256), F32),
            pltpu.VMEM((ROWS, 128), F32),
            pltpu.VMEM((8, ROWS, 256), BF16),
            pltpu.VMEM((SLOTS, PAGE, 2 * HD), BF16),
            pltpu.VMEM((2, FFL, D), BF16),
            pltpu.VMEM((FFL, D), BF16),
            pltpu.VMEM((H * ROWS, HD), BF16),
            pltpu.VMEM((128, HD), BF16),
            pltpu.VMEM((128, HD), BF16),
            pltpu.VMEM((ROWS, 2 * HD), BF16),
            pltpu.VMEM((8, H * ROWS, 256), F32),
            pltpu.VMEM((H * ROWS, 128), F32),
            pltpu.VMEM((H * ROWS, 128), F32),
            pltpu.VMEM((H * ROWS, 128), F32),
            pltpu.VMEM((H * ROWS, HD), F32),
            pltpu.VMEM((8, 4, 8, CB + 128), BF16),
            pltpu.VMEM((NS, 8, CB + 128), BF16),
            pltpu.VMEM((128, CB), BF16),
            pltpu.VMEM((2, 16, 8, CB), BF16),
            pltpu.VMEM((2, 16, ROWS, 128), BF16),
            pltpu.VMEM((8, 4, 8, CB), F32),
            pltpu.VMEM((8, 4, 8, CB), BF16),
            pltpu.VMEM((NS, 8, CB), BF16),
            dma((3,)),
            dma((2, 4, 2)),
            dma((2, 4, 2)),
            dma((2, 4, 2)),
            dma((2, 4, 2)),
            dma((6,)),
            dma((6,)),
            dma((6, 15)),
            dma((6,)),
        ],
        compiler_params=pltpu.CompilerParams(
            collective_id=0, has_side_effects=True, vmem_limit_bytes=60 * 1024 * 1024
        ),
        name="layer",
    )(
        tokens,
        attn_gain.reshape(D // 128, 128),
        qkv_weight,
        out_weight,
        mlp_gain.reshape(D // 128, 128),
        gate_up,
        down_weight,
        kv_pool,
        cache_len,
        page_table,
        inverse,
    )
    return (blocks.reshape(R, NEW, D), written_pool)


def solution(mesh):
    in_specs = (
        P("dp", None, None),
        P(),
        P(("seq", "dp"), None),
        P(("seq", "dp"), None),
        P(),
        P(None, "seq", None),
        P("seq", None),
        P(("dp", "seq"), None, None),
        P("dp"),
        P("dp", None),
    )
    out_specs = (P("dp", None, None), P(("dp", "seq"), None, None))
    return jax.shard_map(body, mesh=mesh, in_specs=in_specs, out_specs=out_specs, check_vma=False)
```
